512 devices in a mesh: section: 4 (over x), expert: 128 (over y, z, core).
Axes of the slice: x: 4, y: 8, z: 8, core: 2. Of those that a mesh axis runs over, the one named last changes fastest.
Arguments:
- activations: bfloat16 [4, 2, 256, 3072], P('section', None, 'expert'), may hold values from -6 to 6
- routes: int32 [4, 2, 256, 2], P('section', None, 'expert'), may hold values from 0 to 3, all different within a row; in each aligned block of 2 rows (0 to 1, 2 to 3, ..., all dimensions but the last counted through in order) at most 2 rows name the same one
- gate_weights: float32 [4, 2, 256, 2], P('section', None, 'expert'), may hold values from 0.1 to 1
- w_gate: bfloat16 [4, 3072, 32768], P('section', None, 'expert'), may hold values from -0.109375 to 0.109375
- w_up: bfloat16 [4, 3072, 32768], P('section', None, 'expert'), may hold values from -0.109375 to 0.109375
- w_down: bfloat16 [4, 32768, 3072], P('section', 'expert'), may hold values from -0.0625 to 0.0625
Outputs:
- received: bfloat16 [4, 2, 256, 3072], P('section', None, 'expert')
The draws below stay inside these ranges and needn't reach their ends.
Inputs may be any that keep to these rules, and one draw needn't show every extreme that they name: `routes`: each token names two different experts. Among the 2 tokens of one block of one section and micro-batch, at most 2 name any one expert, and in every draw some block has exactly 2 naming one expert.
All inputs are finite; a program needn't handle non-finite values.
Results may differ from the reference program's by a relative error of at most 0.005.
Values may be sent and summed in bfloat16 or wider, within the bound.
A program may use at most 64 MiB of HBM per device.

```python
import math
import jax
import jax.numpy as jnp
import numpy as np
from jax import lax

D = 3072
FF = 8192
EXPERTS = 4
MICRO = 2
TOK_MB = 2
CAP = 2
HID = 256
GROUP = 32
SLOTS = 256
TOKENS = 256
SECTIONS = 4
N_EXPERT = 128


def level_of(own_key, dims, split, least, top_value):
    gain, own = 1.0, jax.random.fold_in(own_key, 6)
    for dim, parts in split:
        draws = jnp.exp(jax.random.uniform(jax.random.fold_in(own, dim), (parts,), jnp.float32, least / len(split), top_value / len(split)))
        gain = gain * jnp.repeat(draws, dims[dim] // parts).reshape([-1 if axis == dim else 1 for axis in range(len(dims))])
    return gain


def shared_out(rng, own, number, rows, count, top, reach, lean):
    sequence = jax.random.permutation(rng, count)
    crowded, usual = load_shares(count, rows * top, reach, lean, True), load_shares(count, rows * top, reach, lean, False)
    places = jnp.arange(count)

    def named(lengths, turn):
        used = int((lengths > 0).sum())
        fixed = max(1, used // 4)
        moved = fixed + (places - fixed + turn * (used - fixed)) % max(1, count - fixed)
        return jnp.zeros((count,), jnp.int32).at[sequence[jnp.where(places < fixed, places, moved)]].set(jnp.asarray(lengths, jnp.int32))

    lengths = jnp.where(number % 4 == 0, named(crowded, number // 4), named(usual, number - number // 4 - 1))
    mixed = jax.random.permutation(jax.random.fold_in(own, 3), count)
    source_of, receiver = mixed[0:count // 2 * 2:2], mixed[1:count // 2 * 2:2]
    slack = jnp.minimum(lengths[source_of] - 1, reach - lengths[receiver]) // 2
    slack = jnp.where((source_of == sequence[0]) | (receiver == sequence[0]) | (lengths[receiver] == 0), 0, jnp.maximum(slack, 0))
    moved = jax.random.randint(jax.random.fold_in(own, 4), (count // 2,), 0, 1 << 20) % (slack + 1)
    lengths = lengths.at[source_of].add(-moved).at[receiver].add(moved)
    members = jnp.searchsorted(jnp.cumsum(lengths), jnp.arange(rows * top), side="right").astype(jnp.int32)
    grid = members.reshape(top, rows).T
    grid = grid[jax.random.permutation(jax.random.fold_in(own, 1), rows)]
    turn = jax.random.randint(jax.random.fold_in(own, 2), (rows, 1), 0, top)
    return jnp.take_along_axis(grid, (jnp.arange(top)[None, :] + turn) % top, axis=1)


def load_shares(number_of, total, most, slope, full):
    weights = [(1 << 20) // math.isqrt(rank ** slope) + 1 for rank in range(1, number_of + 1)]
    largest = most if full else min(most, max(-(-total // number_of), total * weights[0] // sum(weights)))
    least = 1 if total - largest >= number_of - 1 else 0
    counts, surplus = [largest] + [least] * (number_of - 1), total - largest - least * (number_of - 1)
    while surplus > 0:
        candidates = [i for i in range(1, number_of) if counts[i] < largest] or [i for i in range(1, number_of) if counts[i] < most]
        pool, left = sum([weights[i] for i in candidates]), surplus
        for i in candidates:
            addition = min(most - counts[i], max(1, left * weights[i] // pool), surplus)
            counts[i] = counts[i] + addition
            surplus = surplus - addition
    return np.array(counts)


def noise(stream_key, extent, spread, reach, cuts=(), kind=jnp.bfloat16):
    drawn = spread * jax.random.normal(stream_key, extent, jnp.float32)
    if cuts:
        drawn = drawn * level_of(stream_key, extent, cuts, -0.22, 0.18)
    return jnp.clip(drawn, -reach, reach).astype(kind)


def setup_inputs(seed: int = 0) -> dict:
    arg_keys = jax.random.split(jax.random.key(seed), 7)
    activations = noise(arg_keys[0], (SECTIONS, MICRO, TOKENS, D), 1.0, 6.0, ((0, 4), (2, 128)))
    routes_keys = jax.random.split(jax.random.fold_in(arg_keys[1], 1), SECTIONS * MICRO * TOKENS // TOK_MB)
    routes_turns = jax.random.permutation(jax.random.fold_in(arg_keys[1], 3), SECTIONS * MICRO * TOKENS // TOK_MB)
    routes = jax.vmap(lambda own, number: shared_out(jax.random.fold_in(arg_keys[1], 2), own, number, TOK_MB, EXPERTS, 2, CAP, 2))(routes_keys, routes_turns).reshape((SECTIONS, MICRO, TOKENS, 2))
    gate_weights = jnp.clip(jnp.exp(math.log(1.0) - 2.3025851 * jax.random.uniform(arg_keys[2], (SECTIONS, MICRO, TOKENS, 2), jnp.float32) ** level_of(arg_keys[2], (SECTIONS, MICRO, TOKENS, 2), ((0, 4), (2, 128)), -0.2, 0.2)), 0.1, 1.0)
    w_gate = noise(arg_keys[3], (SECTIONS, D, EXPERTS * FF), D ** -0.5, 0.109375, ((0, 4), (2, 128)))
    w_up = noise(arg_keys[4], (SECTIONS, D, EXPERTS * FF), D ** -0.5, 0.109375, ((0, 4), (2, 128)))
    w_down = noise(arg_keys[5], (SECTIONS, EXPERTS * FF, D), FF ** -0.5, 0.0625, ((0, 4), (1, 128)))
    return dict(activations=activations, routes=routes, gate_weights=gate_weights, w_gate=w_gate, w_up=w_up, w_down=w_down)


def expert_block(operands):
    buffer, gate_cols, up_cols, down_rows = operands
    gate_proj = jnp.dot(buffer, gate_cols, preferred_element_type=jnp.float32)
    up_proj = jnp.dot(buffer, up_cols, preferred_element_type=jnp.float32)
    hidden = (jax.nn.silu(gate_proj) * up_proj).astype(jnp.bfloat16)
    blocks = hidden.reshape(buffer.shape[0], GROUP, HID).transpose(1, 0, 2)
    down_blocks = down_rows.reshape(GROUP, HID, down_rows.shape[-1])

    def add_block(running, pieces):
        piece_out = jnp.dot(pieces[0], pieces[1], preferred_element_type=jnp.float32).astype(jnp.bfloat16)
        piece_out = lax.optimization_barrier(piece_out)
        return running + piece_out.astype(jnp.float32), None

    start = jnp.zeros((buffer.shape[0], down_rows.shape[-1]), jnp.float32)
    running, _ = lax.scan(add_block, start, (blocks, down_blocks))
    return running


def moe_layer(tok_rows, route_rows, weight_rows, gate_all, up_all, down_all):
    expert_ids = jnp.arange(EXPERTS, dtype=jnp.int32)
    onehot = (route_rows[:, :, None] == expert_ids[None, None, :]).astype(jnp.int32)
    member = jnp.sum(onehot, axis=1).reshape(N_EXPERT, TOK_MB, EXPERTS)
    before = (jnp.cumsum(member, axis=1) - member).reshape(TOKENS, EXPERTS)
    position = jnp.sum(onehot * before[:, None, :], axis=2)
    block_index = jnp.arange(TOKENS, dtype=jnp.int32) // TOK_MB
    slot_row = (block_index[:, None] * CAP + position).astype(jnp.int32)
    buffer = jnp.zeros((EXPERTS, SLOTS, D), tok_rows.dtype)
    buffer = buffer.at[route_rows[:, 0], slot_row[:, 0]].set(tok_rows)
    buffer = buffer.at[route_rows[:, 1], slot_row[:, 1]].set(tok_rows)
    gate_cols = gate_all.reshape(D, EXPERTS, FF).transpose(1, 0, 2)
    up_cols = up_all.reshape(D, EXPERTS, FF).transpose(1, 0, 2)
    down_rows = down_all.reshape(EXPERTS, FF, D)
    expert_outs = lax.map(expert_block, (buffer, gate_cols, up_cols, down_rows))
    picked = expert_outs[route_rows, slot_row]
    mixed_rows = tok_rows.astype(jnp.float32) + jnp.sum(weight_rows[:, :, None] * picked, axis=1)
    return mixed_rows.astype(jnp.bfloat16)


def reference(activations, routes, gate_weights, w_gate, w_up, w_down):
    section_list = []
    for section_index in range(SECTIONS):
        micro_list = []
        for micro_index in range(MICRO):
            micro_list.append(moe_layer(activations[section_index, micro_index], routes[section_index, micro_index],
                                        gate_weights[section_index, micro_index], w_gate[section_index],
                                        w_up[section_index], w_down[section_index]))
        section_list.append(jnp.stack(micro_list))
    stacked = jnp.stack(section_list)
    return jnp.roll(stacked, 1, axis=0)
```

```python
import jax
import jax.numpy as jnp
from jax import lax
from jax.experimental import pallas as pl
from jax.experimental.pallas import tpu as pltpu
from jax.sharding import PartitionSpec as P

EXPERTS = 4
MICRO = 2
ROWS = 2
D = 3072
HID = 256
RING = 8
LANES = 128
TILES = D // LANES
WIDE = TILES + 1
UNIT = RING * ROWS
SLOT = {0: 0, 1: 1, -1: 2, 2: 3, -2: 4, 3: 5, -3: 6, 4: 7, -4: 7}
MESH = pl.DeviceIdType.MESH
F32 = jnp.float32
BF16 = jnp.bfloat16


def layer_kernel(own_ref, gate_hbm, up_hbm, down_hbm, out_ref,
                 xb, xr, gate_w, up_w, down_w, hid, part, recv, summed, back, final,
                 w_sem, ws_sem, wr_sem, fs_sem, fr_sem, as_sem, ar_sem,
                 rs_sem, rr_sem, bs_sem, br_sem, xs_sem, xr_sem, own_sem):
    section = lax.axis_index("section")
    place = lax.axis_index("expert")
    core = lax.rem(place, 2)
    z = lax.rem(place // 2, RING)
    y = place // (2 * RING)
    first = core == 0
    f_pos = z * (1 - core) + y * core
    g_pos = y * (1 - core) + z * core
    f_step = 1 + (RING - 1) * core
    g_step = RING - (RING - 1) * core
    expert = y // 2

    def at(f, g):
        return (section, (f * f_step + g * g_step) * 2 + core)

    def f_peer(k):
        return at(lax.rem(f_pos + k, RING), g_pos)

    sibling = (section, place + 1 - 2 * core)
    g_next = at(f_pos, lax.rem(g_pos + 1, RING))
    g_prev = at(f_pos, lax.rem(g_pos + RING - 1, RING))
    x_next = (lax.rem(section + 1, 4), place)
    x_prev = (lax.rem(section + 3, 4), place)

    hbm = (gate_hbm, up_hbm, down_hbm)
    held = (gate_w, up_w, down_w)
    own_copies = [pltpu.make_async_copy(hbm[i], held[i].at[0], w_sem.at[i]) for i in range(3)]
    for copy in own_copies:
        copy.start()
    own_block = [pltpu.make_async_copy(own_ref.at[m], xb.at[0, m, :, f_pos], own_sem.at[m]) for m in range(MICRO)]
    for copy in own_block:
        copy.start()

    barrier = pltpu.get_barrier_semaphore()
    partners = [f_peer(k) for k in range(1, RING)] + [g_next, g_prev, sibling, x_next, x_prev]
    for partner in partners:
        pl.semaphore_signal(barrier, inc=1, device_id=partner, device_id_type=MESH)
    pl.semaphore_wait(barrier, len(partners))

    f_out = []
    for m in range(MICRO):
        for k in (4, 3, 5, 2, 6, 1, 7):
            copy = pltpu.make_async_remote_copy(
                src_ref=own_ref.at[m], dst_ref=xb.at[0, m, :, f_pos],
                send_sem=fs_sem.at[m, k], recv_sem=fr_sem.at[m, k],
                device_id=f_peer(k), device_id_type=MESH)
            copy.start()
            f_out.append(copy)
    w_out = []
    for i in range(3):
        copy = pltpu.make_async_remote_copy(
            src_ref=hbm[i], dst_ref=held[i].at[1], send_sem=ws_sem.at[i], recv_sem=wr_sem.at[i],
            device_id=sibling, device_id_type=MESH)
        copy.start()
        w_out.append(copy)

    def g_copy(way, step, m):
        src = SLOT[-step * way]
        dst = SLOT[-(step + 1) * way]
        j = 0 if way == 1 else 1
        return pltpu.make_async_remote_copy(
            src_ref=xb.at[src, m], dst_ref=xb.at[dst, m],
            send_sem=as_sem.at[j, step, m], recv_sem=ar_sem.at[j, step, m],
            device_id=g_next if way == 1 else g_prev, device_id_type=MESH)

    def widen(slot, m):
        view = xb.at[slot, m].reshape(WIDE, UNIT, LANES)
        row = (slot * MICRO + m) * UNIT
        for t in range(WIDE):
            xr[row:row + UNIT, t * LANES:(t + 1) * LANES] = view[t]

    pick = lax.broadcasted_iota(jnp.int32, (LANES, HID), 0)
    pick = jnp.where((pick == expert) | (pick == expert + EXPERTS), 1.0, 0.0).astype(BF16)

    def compute(low, high):
        rows = slice(low * MICRO * UNIT, high * MICRO * UNIT)
        weight = jnp.dot(xr[rows, D:], pick, preferred_element_type=F32)
        for side in range(2):
            gate = jnp.dot(xr[rows, :D], gate_w[side], preferred_element_type=F32)
            up = jnp.dot(xr[rows, :D], up_w[side], preferred_element_type=F32)
            value = gate / (1.0 + jnp.exp(-gate)) * up * weight
            hid[rows, side * HID:(side + 1) * HID] = value.astype(BF16)
        for t in range(D // 256):
            cols = slice(t * 256, (t + 1) * 256)
            total = jnp.dot(hid[rows, :HID], down_w[0, :, cols], preferred_element_type=F32)
            total = total + jnp.dot(hid[rows, HID:], down_w[1, :, cols], preferred_element_type=F32)
            part[rows, cols] = total.astype(BF16)

    g_out = []
    for m in range(MICRO):
        own_block[m].wait()
        for k in range(1, RING):
            pltpu.make_async_remote_copy(
                src_ref=own_ref.at[m], dst_ref=xb.at[0, m, :, f_pos],
                send_sem=fs_sem.at[m, k], recv_sem=fr_sem.at[m, k],
                device_id=f_peer(k), device_id_type=MESH).wait_recv()
        for way in (1, -1):
            copy = g_copy(way, 0, m)
            copy.start()
            g_out.append(copy)
    for m in range(MICRO):
        widen(0, m)
    for step in range(1, 4):
        for m in range(MICRO):
            for way in (1, -1):
                g_copy(way, step - 1, m).wait_recv()
                if step < 3 or m == (0 if way == 1 else 1):
                    copy = g_copy(way, step, m)
                    copy.start()
                    g_out.append(copy)
        for m in range(MICRO):
            for way in (1, -1):
                widen(SLOT[-step * way], m)
        if step == 2:
            for i in range(3):
                own_copies[i].wait()
                w_out[i].wait()
            compute(0, 3)
        if step == 3:
            compute(3, 5)
    g_copy(1, 3, 0).wait_recv()
    g_copy(-1, 3, 1).wait_recv()
    for m in range(MICRO):
        widen(SLOT[4], m)
    compute(5, 8)

    def unit(slot, m):
        row = (slot * MICRO + m) * UNIT
        return part.at[row:row + UNIT]

    def back_copy(way, dist, m):
        j = 0 if way == 1 else 1
        return pltpu.make_async_remote_copy(
            src_ref=unit(SLOT[dist * way], m), dst_ref=recv.at[j, dist - 1, m],
            send_sem=rs_sem.at[j, dist - 1, m], recv_sem=rr_sem.at[j, dist - 1, m],
            device_id=g_next if way == 1 else g_prev, device_id_type=MESH)

    for dist in range(4, 0, -1):
        for m in range(MICRO):
            for way in (1, -1):
                j = 0 if way == 1 else 1
                if dist == 4 and m != j:
                    continue
                if dist < 3 or (dist == 3 and m == j):
                    back_copy(way, dist + 1, m).wait_recv()
                    here = unit(SLOT[dist * way], m)
                    here[...] = (here[...].astype(F32) + recv[j, dist, m].astype(F32)).astype(BF16)
                copy = back_copy(way, dist, m)
                copy.start()
                g_out.append(copy)
    for m in range(MICRO):
        back_copy(1, 1, m).wait_recv()
        back_copy(-1, 1, m).wait_recv()
        here = unit(0, m)
        for t in range(TILES):
            cols = slice(t * LANES, (t + 1) * LANES)
            total = here[:, cols].astype(F32) + recv[0, 0, m, :, cols].astype(F32) + recv[1, 0, m, :, cols].astype(F32)
            summed.at[m].reshape(TILES, UNIT, LANES)[t] = total.astype(BF16)

    def f_back(k):
        return pltpu.make_async_remote_copy(
            src_ref=summed.at[:, :, lax.rem(f_pos + k, RING)], dst_ref=back.at[k],
            send_sem=bs_sem.at[k], recv_sem=br_sem.at[k],
            device_id=f_peer(k), device_id_type=MESH)

    for k in (4, 3, 5, 2, 6, 1, 7):
        copy = f_back(k)
        copy.start()
        g_out.append(copy)
    keep = pltpu.make_async_copy(summed.at[:, :, f_pos], back.at[0], br_sem.at[0])
    keep.start()
    keep.wait()
    total = own_ref[:, :TILES].astype(F32) + back[0].astype(F32)
    for k in (1, 7, 2, 6, 3, 5, 4):
        f_back(k).wait_recv()
        total = total + back[k].astype(F32)
    final[...] = total.astype(BF16)
    last = pltpu.make_async_remote_copy(
        src_ref=final, dst_ref=out_ref, send_sem=xs_sem, recv_sem=xr_sem,
        device_id=x_next, device_id_type=MESH)
    last.start()
    for copy in f_out + g_out:
        copy.wait_send()
    last.wait()


def on_device(activations, routes, gate_weights, w_gate, w_up, w_down):
    tokens = activations[0].reshape(MICRO, ROWS, TILES, LANES).transpose(0, 2, 1, 3)
    named = (routes[0][..., None] == jnp.arange(EXPERTS, dtype=jnp.int32)).astype(F32)
    weight = jnp.sum(gate_weights[0][..., None] * named, axis=2)
    high = lax.reduce_precision(weight, 8, 7)
    low = weight - high
    extra = jnp.concatenate([high, low], axis=-1).astype(BF16)
    extra = jnp.pad(extra, ((0, 0), (0, 0), (0, LANES - 2 * EXPERTS)))
    own = jnp.concatenate([tokens, extra[:, None]], axis=1)
    dma = pltpu.SemaphoreType.DMA
    vmem = pltpu.VMEM
    out = pl.pallas_call(
        layer_kernel,
        out_shape=jax.ShapeDtypeStruct((MICRO, TILES, ROWS, LANES), BF16),
        in_specs=[pl.BlockSpec(memory_space=pltpu.VMEM)] + [pl.BlockSpec(memory_space=pl.ANY)] * 3,
        out_specs=pl.BlockSpec(memory_space=pltpu.VMEM),
        scratch_shapes=[
            vmem((RING, MICRO, WIDE, RING, ROWS, LANES), BF16),
            vmem((RING * MICRO * UNIT, WIDE * LANES), BF16),
            vmem((2, D, HID), BF16),
            vmem((2, D, HID), BF16),
            vmem((2, HID, D), BF16),
            vmem((RING * MICRO * UNIT, 2 * HID), BF16),
            vmem((RING * MICRO * UNIT, D), BF16),
            vmem((2, 4, MICRO, UNIT, D), BF16),
            vmem((MICRO, TILES, RING, ROWS, LANES), BF16),
            vmem((RING, MICRO, TILES, ROWS, LANES), BF16),
            vmem((MICRO, TILES, ROWS, LANES), BF16),
            dma((3,)), dma((3,)), dma((3,)),
            dma((MICRO, RING)), dma((MICRO, RING)),
            dma((2, 4, MICRO)), dma((2, 4, MICRO)),
            dma((2, 4, MICRO)), dma((2, 4, MICRO)),
            dma((RING,)), dma((RING,)),
            dma, dma, dma((MICRO,)),
        ],
        compiler_params=pltpu.CompilerParams(
            collective_id=0, has_side_effects=True, vmem_limit_bytes=56 << 20),
    )(own, w_gate[0], w_up[0], w_down[0])
    return out.transpose(0, 2, 1, 3).reshape(1, MICRO, ROWS, D)


def solution(mesh):
    placed = (
        P("section", None, "expert", None),
        P("section", None, "expert", None),
        P("section", None, "expert", None),
        P("section", None, "expert"),
        P("section", None, "expert"),
        P("section", "expert", None),
    )
    return jax.shard_map(
        on_device,
        mesh=mesh,
        in_specs=placed,
        out_specs=P("section", None, "expert", None),
        check_vma=False,
    )
```

```python
import jax
import jax.numpy as jnp
from jax import lax
from jax.experimental import pallas as pl
from jax.experimental.pallas import tpu as pltpu
from jax.sharding import PartitionSpec as P

EXPERTS = 4
MICRO = 2
ROWS = 2
D = 3072
HID = 256
RING = 8
LANES = 128
TILES = D // LANES
WIDE = TILES + 1
UNIT = RING * ROWS
SLOT = {0: 0, 1: 1, -1: 2, 2: 3, -2: 4, 3: 5, -3: 6, 4: 7, -4: 7}
MESH = pl.DeviceIdType.MESH
F32 = jnp.float32
BF16 = jnp.bfloat16


ORDER = (0, 1, 7, 2, 6, 3, 5, 4)
SEAT = {k: i for i, k in enumerate(ORDER)}
GROUPS = ((0, 1), (1, 3), (3, 5), (5, 8))
WAYS = (1, -1)
HALF = RING * UNIT


def layer_kernel(act_hbm, routes_ref, weights_ref, gate_hbm, up_hbm, down_hbm, out_ref,
                 xb, xr, gate_w, up_w, down_w, hid, part, recv, summed, back, final,
                 w_sem, ws_sem, wr_sem, fs_sem, fr_sem, as_sem, ar_sem,
                 rs_sem, rr_sem, bs_sem, br_sem, xs_sem, xr_sem, own_sem):
    section = lax.axis_index("section")
    place = lax.axis_index("expert")
    core = lax.rem(place, 2)
    z = lax.rem(place // 2, RING)
    y = place // (2 * RING)
    f_pos = z * (1 - core) + y * core
    g_pos = y * (1 - core) + z * core
    f_step = 1 + (RING - 1) * core
    g_step = RING - (RING - 1) * core
    expert = y // 2

    def at(f, g):
        return (section, (f * f_step + g * g_step) * 2 + core)

    def f_peer(k):
        return at(lax.rem(f_pos + k, RING), g_pos)

    def g_peer(k):
        return at(f_pos, lax.rem(g_pos + RING + k, RING))

    sibling = (section, place + 1 - 2 * core)
    x_next = (lax.rem(section + 1, 4), place)
    x_prev = (lax.rem(section + 3, 4), place)

    barrier = pltpu.get_barrier_semaphore()
    partners = [f_peer(k) for k in range(1, RING)] + [g_peer(k) for k in (1, -1, 2, -2)] + [sibling, x_next, x_prev]
    for partner in partners:
        pl.semaphore_signal(barrier, inc=1, device_id=partner, device_id_type=MESH)

    hbm = (gate_hbm, up_hbm, down_hbm)
    held = (gate_w, up_w, down_w)
    own_block = pltpu.make_async_copy(act_hbm, xb.at[0, :, 0:TILES, 0], own_sem)
    own_block.start()
    own_copies = [pltpu.make_async_copy(hbm[i], held[i].at[0], w_sem.at[i]) for i in range(3)]
    for copy in own_copies:
        copy.start()
    lane = lax.broadcasted_iota(jnp.int32, (ROWS, LANES), 1)
    for m in range(MICRO):
        weight = jnp.zeros((ROWS, LANES), F32)
        for k in range(2):
            named = (lax.rem(lane, EXPERTS) == routes_ref[m, :, k:k + 1]) & (lane < 2 * EXPERTS)
            weight = weight + jnp.where(named, weights_ref[m, :, k:k + 1], 0.0)
        high = weight.astype(BF16)
        low = (weight - high.astype(F32)).astype(BF16)
        xb[0, m, TILES, 0] = jnp.where(lane < EXPERTS, high.astype(F32), low.astype(F32)).astype(BF16)
    own_block.wait()
    pl.semaphore_wait(barrier, len(partners))

    def f_copy(m, k):
        return pltpu.make_async_remote_copy(
            src_ref=xb.at[0, m, :, 0], dst_ref=xb.at[0, m, :, SEAT[RING - k]],
            send_sem=fs_sem.at[m, k], recv_sem=fr_sem.at[m, RING - k],
            device_id=f_peer(k), device_id_type=MESH)

    def f_wait(m, k):
        pltpu.make_async_remote_copy(
            src_ref=xb.at[0, m, :, 0], dst_ref=xb.at[0, m, :, SEAT[k]],
            send_sem=fs_sem.at[m, k], recv_sem=fr_sem.at[m, k],
            device_id=f_peer(k), device_id_type=MESH).wait_recv()

    sent = []

    def start(copy):
        copy.start()
        sent.append(copy)

    def g_copy(way, dist, m, group):
        low, high = GROUPS[group]
        j = 0 if way == 1 else 1
        hops = 2 if dist == 4 else 1
        return pltpu.make_async_remote_copy(
            src_ref=xb.at[SLOT[-(dist - hops) * way], m, :, low:high],
            dst_ref=xb.at[SLOT[-dist * way], m, :, low:high],
            send_sem=as_sem.at[j, dist - 1, m, group], recv_sem=ar_sem.at[j, dist - 1, m, group],
            device_id=g_peer(hops * way), device_id_type=MESH)

    def far(way, m):
        return m == (0 if way == 1 else 1)

    def spread(group):
        for m in range(MICRO):
            for way in WAYS:
                start(g_copy(way, 1, m, group))

    def relay(dist, group):
        for m in range(MICRO):
            for way in WAYS:
                g_copy(way, dist, m, group).wait_recv()
                if dist == 2 and far(way, m):
                    start(g_copy(way, 4, m, group))
                start(g_copy(way, dist + 1, m, group))

    def widen(slot, m):
        view = xb.at[slot, m].reshape(WIDE, UNIT, LANES)
        row = m * HALF + slot * UNIT
        for t in range(WIDE):
            xr[row:row + UNIT, t * LANES:(t + 1) * LANES] = view[t]

    pick = lax.broadcasted_iota(jnp.int32, (LANES, HID), 0)
    pick = jnp.where((pick == expert) | (pick == expert + EXPERTS), 1.0, 0.0).astype(BF16)

    def compute(m, low, high):
        rows = slice(m * HALF + low * UNIT, m * HALF + high * UNIT)
        weight = jnp.dot(xr[rows, D:], pick, preferred_element_type=F32)
        for side in range(2):
            gate = jnp.dot(xr[rows, :D], gate_w[side], preferred_element_type=F32)
            up = jnp.dot(xr[rows, :D], up_w[side], preferred_element_type=F32)
            value = gate / (1.0 + jnp.exp(-gate)) * up * weight
            hid[rows, side * HID:(side + 1) * HID] = value.astype(BF16)
        for t in range(D // 256):
            cols = slice(t * 256, (t + 1) * 256)
            total = jnp.dot(hid[rows, :HID], down_w[0, :, cols], preferred_element_type=F32)
            total = total + jnp.dot(hid[rows, HID:], down_w[1, :, cols], preferred_element_type=F32)
            part[rows, cols] = total.astype(BF16)

    for m in range(MICRO):
        for k in (4, 3, 5, 2, 6, 1, 7):
            start(f_copy(m, k))
    spread(0)
    w_out = []
    for i in range(3):
        copy = pltpu.make_async_remote_copy(
            src_ref=hbm[i], dst_ref=held[i].at[1], send_sem=ws_sem.at[i], recv_sem=wr_sem.at[i],
            device_id=sibling, device_id_type=MESH)
        copy.start()
        w_out.append(copy)

    def spread_from(group):
        for m in range(MICRO):
            for i in range(*GROUPS[group]):
                f_wait(m, ORDER[i])
            for way in WAYS:
                start(g_copy(way, 1, m, group))

    spread_from(1)
    relay(1, 0)
    spread_from(2)
    relay(1, 1)
    spread_from(3)
    relay(2, 0)
    relay(1, 2)
    relay(2, 1)
    relay(1, 3)
    relay(2, 2)
    relay(2, 3)
    for i in range(3):
        own_copies[i].wait()
        w_out[i].wait()
    for m in range(MICRO):
        for slot in range(5):
            widen(slot, m)
        compute(m, 0, 5)

    def unit(slot, m):
        row = m * HALF + slot * UNIT
        return part.at[row:row + UNIT]

    def back_copy(way, dist, m):
        j = 0 if way == 1 else 1
        return pltpu.make_async_remote_copy(
            src_ref=unit(SLOT[dist * way], m), dst_ref=recv.at[j, dist - 1, m],
            send_sem=rs_sem.at[j, dist - 1, m], recv_sem=rr_sem.at[j, dist - 1, m],
            device_id=g_peer(2 * way if dist == 4 else way), device_id_type=MESH)

    for m in range(MICRO):
        for way in WAYS:
            for group in range(4):
                g_copy(way, 3, m, group).wait_recv()
                if far(way, m):
                    g_copy(way, 4, m, group).wait_recv()
        for slot in range(5, 8):
            widen(slot, m)
        compute(m, 5, 8)
        for way in WAYS:
            if far(way, m):
                start(back_copy(way, 4, m))
            start(back_copy(way, 3, m))
    for dist in (2, 1):
        for m in range(MICRO):
            for way in WAYS:
                j = 0 if way == 1 else 1
                back_copy(way, dist + 1, m).wait_recv()
                here = unit(SLOT[dist * way], m)
                total = here[...].astype(F32) + recv[j, dist, m].astype(F32)
                if dist == 2 and far(way, m):
                    back_copy(way, 4, m).wait_recv()
                    total = total + recv[j, 3, m].astype(F32)
                here[...] = total.astype(BF16)
                start(back_copy(way, dist, m))

    def f_back(m, k):
        return pltpu.make_async_remote_copy(
            src_ref=summed.at[m, :, SEAT[k]], dst_ref=back.at[m, :, SEAT[RING - k]],
            send_sem=bs_sem.at[m, k], recv_sem=br_sem.at[m, RING - k],
            device_id=f_peer(k), device_id_type=MESH)

    def f_back_wait(m, k):
        pltpu.make_async_remote_copy(
            src_ref=summed.at[m, :, SEAT[k]], dst_ref=back.at[m, :, SEAT[k]],
            send_sem=bs_sem.at[m, k], recv_sem=br_sem.at[m, k],
            device_id=f_peer(k), device_id_type=MESH).wait_recv()

    for m in range(MICRO):
        back_copy(1, 1, m).wait_recv()
        back_copy(-1, 1, m).wait_recv()
        here = unit(0, m)
        for t in range(TILES):
            cols = slice(t * LANES, (t + 1) * LANES)
            total = here[:, cols].astype(F32) + recv[0, 0, m, :, cols].astype(F32) + recv[1, 0, m, :, cols].astype(F32)
            summed.at[m].reshape(TILES, UNIT, LANES)[t] = total.astype(BF16)
        for k in (4, 3, 5, 2, 6, 1, 7):
            start(f_back(m, k))
    last = [pltpu.make_async_remote_copy(
        src_ref=final.at[m], dst_ref=out_ref.at[m], send_sem=xs_sem.at[m], recv_sem=xr_sem.at[m],
        device_id=x_next, device_id_type=MESH) for m in range(MICRO)]
    for m in range(MICRO):
        total = xb[0, m, 0:TILES, 0].astype(F32) + summed[m, :, 0].astype(F32)
        for k in (1, 7, 2, 6, 3, 5, 4):
            f_back_wait(m, k)
            total = total + back[m, :, SEAT[k]].astype(F32)
        final[m] = total.astype(BF16)
        last[m].start()
    for copy in sent:
        copy.wait_send()
    for m in range(MICRO):
        last[m].wait()


def on_device(activations, routes, gate_weights, w_gate, w_up, w_down):
    tokens = activations[0].reshape(MICRO, ROWS, TILES, LANES).transpose(0, 2, 1, 3)
    dma = pltpu.SemaphoreType.DMA
    vmem = pltpu.VMEM
    out = pl.pallas_call(
        layer_kernel,
        out_shape=jax.ShapeDtypeStruct((MICRO, TILES, ROWS, LANES), BF16),
        in_specs=[pl.BlockSpec(memory_space=pl.ANY)] + [pl.BlockSpec(memory_space=pltpu.VMEM)] * 2
        + [pl.BlockSpec(memory_space=pl.ANY)] * 3,
        out_specs=pl.BlockSpec(memory_space=pltpu.VMEM),
        scratch_shapes=[
            vmem((RING, MICRO, WIDE, RING, ROWS, LANES), BF16),
            vmem((MICRO * HALF, WIDE * LANES), BF16),
            vmem((2, D, HID), BF16),
            vmem((2, D, HID), BF16),
            vmem((2, HID, D), BF16),
            vmem((MICRO * HALF, 2 * HID), BF16),
            vmem((MICRO * HALF, D), BF16),
            vmem((2, 4, MICRO, UNIT, D), BF16),
            vmem((MICRO, TILES, RING, ROWS, LANES), BF16),
            vmem((MICRO, TILES, RING, ROWS, LANES), BF16),
            vmem((MICRO, TILES, ROWS, LANES), BF16),
            dma((3,)), dma((3,)), dma((3,)),
            dma((MICRO, RING)), dma((MICRO, RING)),
            dma((2, 4, MICRO, 4)), dma((2, 4, MICRO, 4)),
            dma((2, 4, MICRO)), dma((2, 4, MICRO)),
            dma((MICRO, RING)), dma((MICRO, RING)),
            dma((MICRO,)), dma((MICRO,)), dma,
        ],
        compiler_params=pltpu.CompilerParams(
            collective_id=0, has_side_effects=True, vmem_limit_bytes=56 << 20),
    )(tokens, routes[0], gate_weights[0], w_gate[0], w_up[0], w_down[0])
    return out.transpose(0, 2, 1, 3).reshape(1, MICRO, ROWS, D)


def solution(mesh):
    placed = (
        P("section", None, "expert", None),
        P("section", None, "expert", None),
        P("section", None, "expert", None),
        P("section", None, "expert"),
        P("section", None, "expert"),
        P("section", "expert", None),
    )
    return jax.shard_map(
        on_device,
        mesh=mesh,
        in_specs=placed,
        out_specs=P("section", None, "expert", None),
        check_vma=False,
    )
```

```python
import jax
import jax.numpy as jnp
from jax import lax
from jax.experimental import pallas as pl
from jax.experimental.pallas import tpu as pltpu
from jax.sharding import PartitionSpec as P

EXPERTS = 4
MICRO = 2
ROWS = 2
D = 3072
HID = 256
RING = 8
LANES = 128
TILES = D // LANES
WIDE = TILES + 1
UNIT = RING * ROWS
SLOT = {0: 0, 1: 1, -1: 2, 2: 3, -2: 4, 3: 5, -3: 6, 4: 7, -4: 7}
MESH = pl.DeviceIdType.MESH
F32 = jnp.float32
BF16 = jnp.bfloat16


ORDER = (0, 1, 7, 2, 6, 3, 5, 4)
SEAT = {k: i for i, k in enumerate(ORDER)}
GROUPS = ((0, 1), (1, 3), (3, 5), (5, 8))
WAYS = (1, -1)
HALF = RING * UNIT


def layer_kernel(act_hbm, routes_ref, weights_ref, gate_hbm, up_hbm, down_hbm, out_ref,
                 xb, xr, gate_w, up_w, down_w, hid, part, recv, summed, back, home, landed,
                 w_sem, ws_sem, wr_sem, fs_sem, fr_sem, as_sem, ar_sem,
                 rs_sem, rr_sem, bs_sem, br_sem, own_sem):
    section = lax.axis_index("section")
    place = lax.axis_index("expert")
    core = lax.rem(place, 2)
    z = lax.rem(place // 2, RING)
    y = place // (2 * RING)
    f_pos = z * (1 - core) + y * core
    g_pos = y * (1 - core) + z * core
    f_step = 1 + (RING - 1) * core
    g_step = RING - (RING - 1) * core
    expert = y // 2

    def at(f, g):
        return (section, (f * f_step + g * g_step) * 2 + core)

    def f_peer(k):
        return at(lax.rem(f_pos + k, RING), g_pos)

    def g_peer(k):
        return at(f_pos, lax.rem(g_pos + RING + k, RING))

    sibling = (section, place + 1 - 2 * core)
    x_next = (lax.rem(section + 1, 4), place)
    x_prev = (lax.rem(section + 3, 4), place)

    barrier = pltpu.get_barrier_semaphore()
    partners = [f_peer(k) for k in range(1, RING)] + [g_peer(k) for k in (1, -1, 2, -2)] + [sibling, x_next, x_prev]
    for partner in partners:
        pl.semaphore_signal(barrier, inc=1, device_id=partner, device_id_type=MESH)

    hbm = (gate_hbm, up_hbm, down_hbm)
    held = (gate_w, up_w, down_w)
    own_block = pltpu.make_async_copy(act_hbm, xb.at[0, :, 0:TILES, 0], own_sem)
    own_block.start()
    own_copies = [pltpu.make_async_copy(hbm[i], held[i].at[0], w_sem.at[i]) for i in range(3)]
    for copy in own_copies:
        copy.start()
    lane = lax.broadcasted_iota(jnp.int32, (ROWS, LANES), 1)
    for m in range(MICRO):
        weight = jnp.zeros((ROWS, LANES), F32)
        for k in range(2):
            named = (lax.rem(lane, EXPERTS) == routes_ref[m, :, k:k + 1]) & (lane < 2 * EXPERTS)
            weight = weight + jnp.where(named, weights_ref[m, :, k:k + 1], 0.0)
        high = weight.astype(BF16)
        low = (weight - high.astype(F32)).astype(BF16)
        xb[0, m, TILES, 0] = jnp.where(lane < EXPERTS, high.astype(F32), low.astype(F32)).astype(BF16)
    own_block.wait()
    pl.semaphore_wait(barrier, len(partners))

    def f_copy(m, k):
        return pltpu.make_async_remote_copy(
            src_ref=xb.at[0, m, :, 0], dst_ref=xb.at[0, m, :, SEAT[RING - k]],
            send_sem=fs_sem.at[m, k], recv_sem=fr_sem.at[m, RING - k],
            device_id=f_peer(k), device_id_type=MESH)

    def f_wait(m, k):
        pltpu.make_async_remote_copy(
            src_ref=xb.at[0, m, :, 0], dst_ref=xb.at[0, m, :, SEAT[k]],
            send_sem=fs_sem.at[m, k], recv_sem=fr_sem.at[m, k],
            device_id=f_peer(k), device_id_type=MESH).wait_recv()

    sent = []

    def start(copy):
        copy.start()
        sent.append(copy)

    def g_copy(way, dist, m, group):
        low, high = GROUPS[group]
        j = 0 if way == 1 else 1
        hops = 2 - dist % 2
        source = 0 if dist <= 2 else 2
        return pltpu.make_async_remote_copy(
            src_ref=xb.at[SLOT[-source * way], m, :, low:high],
            dst_ref=xb.at[SLOT[-dist * way], m, :, low:high],
            send_sem=as_sem.at[j, dist - 1, m, group], recv_sem=ar_sem.at[j, dist - 1, m, group],
            device_id=g_peer(hops * way), device_id_type=MESH)

    def far(way, m):
        return m == (0 if way == 1 else 1)

    def spread(group):
        for m in range(MICRO):
            for dist in (2, 1):
                for way in WAYS:
                    start(g_copy(way, dist, m, group))

    def relay(group):
        for m in range(MICRO):
            for way in WAYS:
                g_copy(way, 2, m, group).wait_recv()
                if far(way, m):
                    start(g_copy(way, 4, m, group))
                start(g_copy(way, 3, m, group))

    def widen(slot, m):
        view = xb.at[slot, m].reshape(WIDE, UNIT, LANES)
        row = m * HALF + slot * UNIT
        for t in range(WIDE):
            xr[row:row + UNIT, t * LANES:(t + 1) * LANES] = view[t]

    pick = lax.broadcasted_iota(jnp.int32, (LANES, HID), 0)
    pick = jnp.where((pick == expert) | (pick == expert + EXPERTS), 1.0, 0.0).astype(BF16)

    def compute(m, low, high):
        rows = slice(m * HALF + low * UNIT, m * HALF + high * UNIT)
        weight = jnp.dot(xr[rows, D:], pick, preferred_element_type=F32)
        for side in range(2):
            gate = jnp.dot(xr[rows, :D], gate_w[side], preferred_element_type=F32)
            up = jnp.dot(xr[rows, :D], up_w[side], preferred_element_type=F32)
            value = gate / (1.0 + jnp.exp(-gate)) * up * weight
            hid[rows, side * HID:(side + 1) * HID] = value.astype(BF16)
        for t in range(D // 256):
            cols = slice(t * 256, (t + 1) * 256)
            total = jnp.dot(hid[rows, :HID], down_w[0, :, cols], preferred_element_type=F32)
            total = total + jnp.dot(hid[rows, HID:], down_w[1, :, cols], preferred_element_type=F32)
            part[rows, cols] = total.astype(BF16)

    for m in range(MICRO):
        for k in (4, 3, 5, 2, 6, 1, 7):
            start(f_copy(m, k))
    spread(0)
    w_out = []
    for i in range(3):
        copy = pltpu.make_async_remote_copy(
            src_ref=hbm[i], dst_ref=held[i].at[1], send_sem=ws_sem.at[i], recv_sem=wr_sem.at[i],
            device_id=sibling, device_id_type=MESH)
        copy.start()
        w_out.append(copy)

    def spread_from(group):
        for m in range(MICRO):
            for i in range(*GROUPS[group]):
                f_wait(m, ORDER[i])
        spread(group)

    spread_from(1)
    relay(0)
    spread_from(2)
    spread_from(3)
    relay(1)
    relay(2)
    relay(3)
    for m in range(MICRO):
        for way in WAYS:
            for group in range(4):
                g_copy(way, 1, m, group).wait_recv()
    def unit(slot, m):
        row = m * HALF + slot * UNIT
        return part.at[row:row + UNIT]

    def back_copy(way, dist, m):
        j = 0 if way == 1 else 1
        return pltpu.make_async_remote_copy(
            src_ref=unit(SLOT[dist * way], m), dst_ref=recv.at[j, dist - 1, m],
            send_sem=rs_sem.at[j, dist - 1, m], recv_sem=rr_sem.at[j, dist - 1, m],
            device_id=g_peer((2 - dist % 2) * way), device_id_type=MESH)

    for i in range(3):
        own_copies[i].wait()
        w_out[i].wait_recv()
    for m in range(MICRO):
        for slot in range(5):
            widen(slot, m)
        compute(m, 0, 5)
        for way in WAYS:
            start(back_copy(way, 1, m))

    for m in range(MICRO):
        for way in WAYS:
            for group in range(4):
                g_copy(way, 3, m, group).wait_recv()
                if far(way, m):
                    g_copy(way, 4, m, group).wait_recv()
        for slot in range(5, 8):
            widen(slot, m)
        compute(m, 5, 8)
        for way in WAYS:
            if far(way, m):
                start(back_copy(way, 4, m))
            start(back_copy(way, 3, m))
    for m in range(MICRO):
        for way in WAYS:
            j = 0 if way == 1 else 1
            back_copy(way, 3, m).wait_recv()
            here = unit(SLOT[2 * way], m)
            total = here[...].astype(F32) + recv[j, 2, m].astype(F32)
            if far(way, m):
                back_copy(way, 4, m).wait_recv()
                total = total + recv[j, 3, m].astype(F32)
            here[...] = total.astype(BF16)
            start(back_copy(way, 2, m))

    def home_copy(m):
        return pltpu.make_async_remote_copy(
            src_ref=home.at[m], dst_ref=landed.at[m], send_sem=bs_sem.at[m, 0], recv_sem=br_sem.at[m, 0],
            device_id=x_next, device_id_type=MESH)

    def f_back(m, k):
        return pltpu.make_async_remote_copy(
            src_ref=summed.at[m, :, SEAT[k]], dst_ref=back.at[m, :, SEAT[RING - k]],
            send_sem=bs_sem.at[m, k], recv_sem=br_sem.at[m, RING - k],
            device_id=(x_next[0], f_peer(k)[1]), device_id_type=MESH)

    def f_back_wait(m, k):
        pltpu.make_async_remote_copy(
            src_ref=summed.at[m, :, SEAT[k]], dst_ref=back.at[m, :, SEAT[k]],
            send_sem=bs_sem.at[m, k], recv_sem=br_sem.at[m, k],
            device_id=(x_next[0], f_peer(k)[1]), device_id_type=MESH).wait_recv()

    for m in range(MICRO):
        for way in WAYS:
            for dist in (1, 2):
                back_copy(way, dist, m).wait_recv()
        here = unit(0, m)
        for t in range(TILES):
            cols = slice(t * LANES, (t + 1) * LANES)
            total = here[:, cols].astype(F32)
            for dist in range(2):
                total = total + recv[0, dist, m, :, cols].astype(F32) + recv[1, dist, m, :, cols].astype(F32)
            home[m, t] = xb[0, m, t, 0].astype(F32) + total[0:ROWS]
            summed.at[m].reshape(TILES, UNIT, LANES)[t] = total.astype(BF16)
        for k in (4, 3, 5, 2, 6, 1, 7):
            start(f_back(m, k))
        start(home_copy(m))
    for m in range(MICRO):
        home_copy(m).wait_recv()
        total = landed[m]
        for k in (1, 7, 2, 6, 3, 5, 4):
            f_back_wait(m, k)
            total = total + back[m, :, SEAT[k]].astype(F32)
        out_ref[m] = total.astype(BF16)
    for copy in sent:
        copy.wait_send()
    for copy in w_out:
        copy.wait_send()


def on_device(activations, routes, gate_weights, w_gate, w_up, w_down):
    tokens = activations[0].reshape(MICRO, ROWS, TILES, LANES).transpose(0, 2, 1, 3)
    dma = pltpu.SemaphoreType.DMA
    vmem = pltpu.VMEM
    out = pl.pallas_call(
        layer_kernel,
        out_shape=jax.ShapeDtypeStruct((MICRO, TILES, ROWS, LANES), BF16),
        in_specs=[pl.BlockSpec(memory_space=pl.ANY)] + [pl.BlockSpec(memory_space=pltpu.VMEM)] * 2
        + [pl.BlockSpec(memory_space=pl.ANY)] * 3,
        out_specs=pl.BlockSpec(memory_space=pltpu.VMEM),
        scratch_shapes=[
            vmem((RING, MICRO, WIDE, RING, ROWS, LANES), BF16),
            vmem((MICRO * HALF, WIDE * LANES), BF16),
            vmem((2, D, HID), BF16),
            vmem((2, D, HID), BF16),
            vmem((2, HID, D), BF16),
            vmem((MICRO * HALF, 2 * HID), BF16),
            vmem((MICRO * HALF, D), BF16),
            vmem((2, 4, MICRO, UNIT, D), BF16),
            vmem((MICRO, TILES, RING, ROWS, LANES), BF16),
            vmem((MICRO, TILES, RING, ROWS, LANES), BF16),
            vmem((MICRO, TILES, ROWS, LANES), F32),
            vmem((MICRO, TILES, ROWS, LANES), F32),
            dma((3,)), dma((3,)), dma((3,)),
            dma((MICRO, RING)), dma((MICRO, RING)),
            dma((2, 4, MICRO, 4)), dma((2, 4, MICRO, 4)),
            dma((2, 4, MICRO)), dma((2, 4, MICRO)),
            dma((MICRO, RING)), dma((MICRO, RING)),
            dma,
        ],
        compiler_params=pltpu.CompilerParams(
            collective_id=0, has_side_effects=True, vmem_limit_bytes=56 << 20),
    )(tokens, routes[0], gate_weights[0], w_gate[0], w_up[0], w_down[0])
    return out.transpose(0, 2, 1, 3).reshape(1, MICRO, ROWS, D)


def solution(mesh):
    placed = (
        P("section", None, "expert", None),
        P("section", None, "expert", None),
        P("section", None, "expert", None),
        P("section", None, "expert"),
        P("section", None, "expert"),
        P("section", "expert", None),
    )
    return jax.shard_map(
        on_device,
        mesh=mesh,
        in_specs=placed,
        out_specs=P("section", None, "expert", None),
        check_vma=False,
    )
```

```python
import jax
import jax.numpy as jnp
from jax import lax
from jax.experimental import pallas as pl
from jax.experimental.pallas import tpu as pltpu
from jax.sharding import PartitionSpec as P

EXPERTS = 4
MICRO = 2
ROWS = 2
D = 3072
HID = 256
RING = 8
LANES = 128
TILES = D // LANES
WIDE = TILES + 1
UNIT = RING * ROWS
SLOT = {0: 0, 1: 1, -1: 2, 2: 3, -2: 4, 3: 5, -3: 6, 4: 7, -4: 7}
MESH = pl.DeviceIdType.MESH
F32 = jnp.float32
BF16 = jnp.bfloat16


ORDER = (0, 1, 7, 2, 6, 3, 5, 4)
SEAT = {k: i for i, k in enumerate(ORDER)}
GROUPS = ((0, 1), (1, 3), (3, 5), (5, 8))
WAYS = (1, -1)
LIGHT = ((1, 1), (0, -1))
HEAVY = ((0, 1), (1, -1))
HALF = RING * UNIT


def layer_kernel(act_hbm, routes_ref, weights_ref, gate_hbm, up_hbm, down_hbm, out_ref,
                 xb, xr, gate_w, up_w, down_w, hid, part, recv, summed, back, home, landed,
                 w_sem, ws_sem, wr_sem, fs_sem, fr_sem, as_sem, ar_sem,
                 rs_sem, rr_sem, bs_sem, br_sem, own_sem):
    section = lax.axis_index("section")
    place = lax.axis_index("expert")
    core = lax.rem(place, 2)
    z = lax.rem(place // 2, RING)
    y = place // (2 * RING)
    f_pos = z * (1 - core) + y * core
    g_pos = y * (1 - core) + z * core
    f_step = 1 + (RING - 1) * core
    g_step = RING - (RING - 1) * core
    expert = y // 2

    def at(f, g):
        return (section, (f * f_step + g * g_step) * 2 + core)

    def f_peer(k):
        return at(lax.rem(f_pos + k, RING), g_pos)

    def g_peer(k):
        return at(f_pos, lax.rem(g_pos + RING + k, RING))

    sibling = (section, place + 1 - 2 * core)
    x_next = (lax.rem(section + 1, 4), place)
    x_prev = (lax.rem(section + 3, 4), place)

    barrier = pltpu.get_barrier_semaphore()
    partners = [f_peer(k) for k in range(1, RING)] + [g_peer(k) for k in (1, -1, 2, -2)] + [sibling, x_next, x_prev]
    for partner in partners:
        pl.semaphore_signal(barrier, inc=1, device_id=partner, device_id_type=MESH)

    hbm = (gate_hbm, up_hbm, down_hbm)
    held = (gate_w, up_w, down_w)
    own_block = pltpu.make_async_copy(act_hbm, xb.at[0, :, 0:TILES, 0], own_sem)
    own_block.start()
    own_copies = [pltpu.make_async_copy(hbm[i], held[i].at[0], w_sem.at[i]) for i in range(3)]
    for copy in own_copies:
        copy.start()
    lane = lax.broadcasted_iota(jnp.int32, (ROWS, LANES), 1)
    for m in range(MICRO):
        weight = jnp.zeros((ROWS, LANES), F32)
        for k in range(2):
            named = (lax.rem(lane, EXPERTS) == routes_ref[m, :, k:k + 1]) & (lane < 2 * EXPERTS)
            weight = weight + jnp.where(named, weights_ref[m, :, k:k + 1], 0.0)
        high = weight.astype(BF16)
        low = (weight - high.astype(F32)).astype(BF16)
        xb[0, m, TILES, 0] = jnp.where(lane < EXPERTS, high.astype(F32), low.astype(F32)).astype(BF16)
    own_block.wait()
    pl.semaphore_wait(barrier, len(partners))

    def f_copy(m, k):
        return pltpu.make_async_remote_copy(
            src_ref=xb.at[0, m, :, 0], dst_ref=xb.at[0, m, :, SEAT[RING - k]],
            send_sem=fs_sem.at[m, k], recv_sem=fr_sem.at[m, RING - k],
            device_id=f_peer(k), device_id_type=MESH)

    def f_wait(m, k):
        pltpu.make_async_remote_copy(
            src_ref=xb.at[0, m, :, 0], dst_ref=xb.at[0, m, :, SEAT[k]],
            send_sem=fs_sem.at[m, k], recv_sem=fr_sem.at[m, k],
            device_id=f_peer(k), device_id_type=MESH).wait_recv()

    sent = []

    def start(copy):
        copy.start()
        sent.append(copy)

    def g_copy(way, dist, m, group):
        low, high = GROUPS[group]
        j = 0 if way == 1 else 1
        near = False
        hops = 1 if near else 2 - dist % 2
        source = 1 if near else 0 if dist <= 2 else 2
        return pltpu.make_async_remote_copy(
            src_ref=xb.at[SLOT[-source * way], m, :, low:high],
            dst_ref=xb.at[SLOT[-dist * way], m, :, low:high],
            send_sem=as_sem.at[j, dist - 1, m, group], recv_sem=ar_sem.at[j, dist - 1, m, group],
            device_id=g_peer(hops * way), device_id_type=MESH)

    def far(way, m):
        return m == (0 if way == 1 else 1)

    def spread(group):
        for dist in (2, 1):
            for m in range(MICRO):
                for way in WAYS:
                    start(g_copy(way, dist, m, group))

    def pass_on(group):
        for m in range(MICRO):
            for way in WAYS:
                g_copy(way, 1, m, group).wait_recv()
                start(g_copy(way, 2, m, group))

    def relay(group):
        for m in range(MICRO):
            for way in WAYS:
                g_copy(way, 2, m, group).wait_recv()
                if far(way, m):
                    start(g_copy(way, 4, m, group))
                start(g_copy(way, 3, m, group))

    def widen(slot, m):
        view = xb.at[slot, m].reshape(WIDE, UNIT, LANES)
        row = (slot * MICRO + m) * UNIT
        for t in range(WIDE):
            xr[row:row + UNIT, t * LANES:(t + 1) * LANES] = view[t]

    pick = lax.broadcasted_iota(jnp.int32, (LANES, HID), 0)
    pick = jnp.where((pick == expert) | (pick == expert + EXPERTS), 1.0, 0.0).astype(BF16)

    def compute(low, high):
        rows = slice(low * MICRO * UNIT, high * MICRO * UNIT)
        weight = jnp.dot(xr[rows, D:], pick, preferred_element_type=F32)
        for side in range(2):
            gate = jnp.dot(xr[rows, :D], gate_w[side], preferred_element_type=F32)
            up = jnp.dot(xr[rows, :D], up_w[side], preferred_element_type=F32)
            value = gate / (1.0 + jnp.exp(-gate)) * up * weight
            hid[rows, side * HID:(side + 1) * HID] = value.astype(BF16)
        for t in range(D // 256):
            cols = slice(t * 256, (t + 1) * 256)
            total = jnp.dot(hid[rows, :HID], down_w[0, :, cols], preferred_element_type=F32)
            total = total + jnp.dot(hid[rows, HID:], down_w[1, :, cols], preferred_element_type=F32)
            part[rows, cols] = total.astype(BF16)

    for m in range(MICRO):
        for k in (4, 3, 5, 2, 6, 1, 7):
            start(f_copy(m, k))
    spread(0)
    w_out = []
    for i in range(3):
        copy = pltpu.make_async_remote_copy(
            src_ref=hbm[i], dst_ref=held[i].at[1], send_sem=ws_sem.at[i], recv_sem=wr_sem.at[i],
            device_id=sibling, device_id_type=MESH)
        copy.start()
        w_out.append(copy)

    def spread_from(group):
        for m in range(MICRO):
            for i in range(*GROUPS[group]):
                f_wait(m, ORDER[i])
        spread(group)

    spread_from(1)
    relay(0)
    spread_from(2)
    spread_from(3)
    relay(1)
    relay(2)
    relay(3)
    for m in range(MICRO):
        for way in WAYS:
            for group in range(4):
                g_copy(way, 1, m, group).wait_recv()
    def unit(slot, m):
        row = (slot * MICRO + m) * UNIT
        return part.at[row:row + UNIT]

    def back_copy(way, dist, m):
        j = 0 if way == 1 else 1
        return pltpu.make_async_remote_copy(
            src_ref=unit(SLOT[dist * way], m), dst_ref=recv.at[j, dist - 1, m],
            send_sem=rs_sem.at[j, dist - 1, m], recv_sem=rr_sem.at[j, dist - 1, m],
            device_id=g_peer((2 - dist % 2) * way), device_id_type=MESH)

    for i in range(3):
        own_copies[i].wait()
        w_out[i].wait_recv()
    for m in range(MICRO):
        for slot in range(5):
            widen(slot, m)
    compute(0, 5)
    for m in range(MICRO):
        for way in WAYS:
            start(back_copy(way, 1, m))

    for m in range(MICRO):
        for way in WAYS:
            for group in range(4):
                g_copy(way, 3, m, group).wait_recv()
                if far(way, m):
                    g_copy(way, 4, m, group).wait_recv()
        for slot in range(5, 8):
            widen(slot, m)
    compute(5, 8)
    for m, way in LIGHT + HEAVY:
        if far(way, m):
            start(back_copy(way, 4, m))
        start(back_copy(way, 3, m))
    for m, way in LIGHT + HEAVY:
        j = 0 if way == 1 else 1
        back_copy(way, 3, m).wait_recv()
        here = unit(SLOT[2 * way], m)
        total = here[...].astype(F32) + recv[j, 2, m].astype(F32)
        if far(way, m):
            back_copy(way, 4, m).wait_recv()
            total = total + recv[j, 3, m].astype(F32)
        here[...] = total.astype(BF16)
        start(back_copy(way, 2, m))

    def home_copy(m):
        return pltpu.make_async_remote_copy(
            src_ref=home.at[m], dst_ref=landed.at[m], send_sem=bs_sem.at[m, 0], recv_sem=br_sem.at[m, 0],
            device_id=x_next, device_id_type=MESH)

    def f_back(m, k):
        return pltpu.make_async_remote_copy(
            src_ref=summed.at[m, :, SEAT[k]], dst_ref=back.at[m, SEAT[RING - k]],
            send_sem=bs_sem.at[m, k], recv_sem=br_sem.at[m, RING - k],
            device_id=(x_next[0], f_peer(k)[1]), device_id_type=MESH)

    def f_back_wait(m, k):
        pltpu.make_async_remote_copy(
            src_ref=summed.at[m, :, SEAT[k]], dst_ref=back.at[m, SEAT[k]],
            send_sem=bs_sem.at[m, k], recv_sem=br_sem.at[m, k],
            device_id=(x_next[0], f_peer(k)[1]), device_id_type=MESH).wait_recv()

    for m in range(MICRO):
        for way in WAYS:
            for dist in (1, 2):
                back_copy(way, dist, m).wait_recv()
        here = unit(0, m)
        for t in range(TILES):
            cols = slice(t * LANES, (t + 1) * LANES)
            total = here[:, cols].astype(F32)
            for dist in range(2):
                total = total + recv[0, dist, m, :, cols].astype(F32) + recv[1, dist, m, :, cols].astype(F32)
            home[m, t] = xb[0, m, t, 0].astype(F32) + total[0:ROWS]
            summed.at[m].reshape(TILES, UNIT, LANES)[t] = total.astype(BF16)
        for k in (4, 3, 5, 2, 6, 1, 7):
            start(f_back(m, k))
        start(home_copy(m))
    for m in range(MICRO):
        home_copy(m).wait_recv()
        total = landed.at[m].reshape(TILES * ROWS, LANES)[...]
        for k in (1, 7, 2, 6, 3, 5, 4):
            f_back_wait(m, k)
            total = total + back.at[m, SEAT[k]].reshape(TILES * ROWS, LANES)[...].astype(F32)
        out_ref[m * TILES * ROWS:(m + 1) * TILES * ROWS] = total
    for copy in sent:
        copy.wait_send()
    for copy in w_out:
        copy.wait_send()


def on_device(activations, routes, gate_weights, w_gate, w_up, w_down):
    tokens = activations[0].reshape(MICRO, ROWS, TILES, LANES).transpose(0, 2, 1, 3)
    dma = pltpu.SemaphoreType.DMA
    vmem = pltpu.VMEM
    out = pl.pallas_call(
        layer_kernel,
        out_shape=jax.ShapeDtypeStruct((MICRO * TILES * ROWS, LANES), F32),
        in_specs=[pl.BlockSpec(memory_space=pl.ANY)] + [pl.BlockSpec(memory_space=pltpu.VMEM)] * 2
        + [pl.BlockSpec(memory_space=pl.ANY)] * 3,
        out_specs=pl.BlockSpec(memory_space=pltpu.VMEM),
        scratch_shapes=[
            vmem((RING, MICRO, WIDE, RING, ROWS, LANES), BF16),
            vmem((MICRO * HALF, WIDE * LANES), BF16),
            vmem((2, D, HID), BF16),
            vmem((2, D, HID), BF16),
            vmem((2, HID, D), BF16),
            vmem((MICRO * HALF, 2 * HID), BF16),
            vmem((MICRO * HALF, D), BF16),
            vmem((2, 4, MICRO, UNIT, D), BF16),
            vmem((MICRO, TILES, RING, ROWS, LANES), BF16),
            vmem((MICRO, RING, TILES, ROWS, LANES), BF16),
            vmem((MICRO, TILES, ROWS, LANES), F32),
            vmem((MICRO, TILES, ROWS, LANES), F32),
            dma((3,)), dma((3,)), dma((3,)),
            dma((MICRO, RING)), dma((MICRO, RING)),
            dma((2, 4, MICRO, 4)), dma((2, 4, MICRO, 4)),
            dma((2, 4, MICRO)), dma((2, 4, MICRO)),
            dma((MICRO, RING)), dma((MICRO, RING)),
            dma,
        ],
        compiler_params=pltpu.CompilerParams(
            collective_id=0, has_side_effects=True, vmem_limit_bytes=56 << 20),
    )(tokens, routes[0], gate_weights[0], w_gate[0], w_up[0], w_down[0])
    out = out.astype(BF16).reshape(MICRO, TILES, ROWS, LANES)
    return out.transpose(0, 2, 1, 3).reshape(1, MICRO, ROWS, D)


def solution(mesh):
    placed = (
        P("section", None, "expert", None),
        P("section", None, "expert", None),
        P("section", None, "expert", None),
        P("section", None, "expert"),
        P("section", None, "expert"),
        P("section", "expert", None),
    )
    return jax.shard_map(
        on_device,
        mesh=mesh,
        in_specs=placed,
        out_specs=P("section", None, "expert", None),
        check_vma=False,
    )
```
